32 devices in a mesh: dp: 8 (over z, x), tensor: 4 (over y, core).
Axes of the slice: x: 2, y: 2, z: 4, core: 2. Of those that a mesh axis runs over, the one named last changes fastest.
Arguments:
- tokens: bfloat16 [16384, 1024], P(('dp', 'tensor')), may hold values from -6 to 6
- condition: bfloat16 [16, 1024], P('dp'), may hold values from -6 to 6
- ada_weight: bfloat16 [1024, 6144], P(None, 'tensor'), may hold values from -0.1875 to 0.1875
- ada_bias: bfloat16 [6144], P('tensor'), may hold values from -3 to 3
- qkv_weight: bfloat16 [1024, 3, 1024], P(None, None, 'tensor'), may hold values from -0.1875 to 0.1875
- qv_bias: bfloat16 [2, 1024], P(None, 'tensor'), may hold values from -3 to 3
- proj_weight: bfloat16 [1024, 1024], P('tensor'), may hold values from -0.75 to 0.75
- proj_bias: bfloat16 [1024], replicated, may hold values from -3 to 3
- up_weight: bfloat16 [4096, 1024], P('tensor'), may hold values from -0.1875 to 0.1875
- up_bias: bfloat16 [4096], P('tensor'), may hold values from -3 to 3
- down_weight: bfloat16 [4096, 1024], P('tensor'), may hold values from -0.09375 to 0.09375
- down_bias: bfloat16 [1024], replicated, may hold values from -3 to 3
- out_grad: bfloat16 [16384, 1024], P(('dp', 'tensor')), may hold values from -6 to 6
Outputs:
- block_out: bfloat16 [16384, 1024], P(('dp', 'tensor'))
- tokens_grad: float32 [16384, 1024], P(('dp', 'tensor'))
- condition_grad: float32 [16, 1024], P('dp')
- ada_weight_grad: float32 [1024, 6144], P(None, 'tensor')
- ada_bias_grad: float32 [6144], P('tensor')
- qkv_weight_grad: float32 [1024, 3, 1024], P(None, None, 'tensor')
- qv_bias_grad: float32 [2, 1024], P(None, 'tensor')
- proj_weight_grad: float32 [1024, 1024], P('tensor')
- proj_bias_grad: float32 [1024], replicated
- up_weight_grad: float32 [4096, 1024], P('tensor')
- up_bias_grad: float32 [4096], P('tensor')
- down_weight_grad: float32 [4096, 1024], P('tensor')
- down_bias_grad: float32 [1024], replicated
The draws below stay inside these ranges and needn't reach their ends.
All inputs are finite; a program needn't handle non-finite values.
Results may differ from the reference program's by a relative error of at most 0.023.
The reference program's roundings to bfloat16 on the way count: a program that leaves them out, or rounds other values in their place, can miss the bound.
Values may be sent and summed in bfloat16 or wider, within the bound.
No kernel may reach another device: no remote copies, remote signals or barrier semaphores. Data moves between devices by JAX's collectives and lax.ppermute only.
A program may use at most 256 MiB of HBM per device.

```python
import math
import jax
import jax.numpy as jnp
from jax import lax

D = 1024
H = 16
HD = 64
FF = 4096
SEQ = 1024
LAT = 16
TOKENS = 16384


def level_of(key, dims, cuts, least, high):
    def one(axis_at, shards_of):
        draws = jax.random.uniform(jax.random.fold_in(jax.random.fold_in(key, 6), axis_at), (shards_of,), jnp.float32, least / len(cuts), high / len(cuts))
        return jnp.repeat(jnp.exp(draws), dims[axis_at] // shards_of).reshape((-1,) + (1,) * (len(dims) - axis_at - 1))

    loudness = one(*cuts[0])
    for cut in cuts[1:]:
        loudness = loudness * one(*cut)
    return loudness


def normal_values(stream_key, shape, spread, reach, pieces=(), held_as=jnp.bfloat16):
    values = spread * jax.random.normal(stream_key, shape, jnp.float32)
    if pieces:
        values = values * level_of(stream_key, shape, pieces, -0.22, 0.18)
    return jnp.clip(values, -reach, reach).astype(held_as)


def setup_inputs(seed: int = 0) -> dict:
    seeds = jax.random.split(jax.random.key(seed), 14)
    return {
        "tokens": normal_values(seeds[0], (TOKENS, D), 1.0, 6.0, ((0, 32),)),
        "condition": normal_values(seeds[1], (LAT, D), 1.0, 6.0, ((0, 8),)),
        "ada_weight": normal_values(seeds[2], (D, 6 * D), D ** -0.5, 0.1875, ((1, 4),)),
        "ada_bias": normal_values(seeds[3], (6 * D,), 0.5, 3.0, ((0, 4),)),
        "qkv_weight": normal_values(seeds[4], (D, 3, D), D ** -0.5, 0.1875, ((2, 4),)),
        "qv_bias": normal_values(seeds[5], (2, D), 0.5, 3.0, ((1, 4),)),
        "proj_weight": normal_values(seeds[6], (D, D), (D // 16) ** -0.5, 0.75, ((0, 4),)),
        "proj_bias": normal_values(seeds[7], (D,), 0.5, 3.0),
        "up_weight": normal_values(seeds[8], (FF, D), D ** -0.5, 0.1875, ((0, 4),)),
        "up_bias": normal_values(seeds[9], (FF,), 0.5, 3.0, ((0, 4),)),
        "down_weight": normal_values(seeds[10], (FF, D), FF ** -0.5, 0.09375, ((0, 4),)),
        "down_bias": normal_values(seeds[11], (D,), 0.5, 3.0),
        "out_grad": normal_values(seeds[12], (TOKENS, D), 1.0, 6.0, ((0, 32),)),
    }


@jax.custom_vjp
def low(v):
    return lax.optimization_barrier(v.astype(jnp.bfloat16)).astype(jnp.float32)

@jax.custom_vjp
def low_back(v):
    return v

def low_keep(v):
    return (low(v), None)

def low_pass(kept, grad):
    return (grad,)

def back_keep(v):
    return (v, None)

def back_low(kept, grad):
    return (low(grad),)
low.defvjp(low_keep, low_pass)
low_back.defvjp(back_keep, back_low)
highest = lax.Precision.HIGHEST
norm_eps = 1e-06

def norm_rows(values):
    row_mean = lax.optimization_barrier(jnp.mean(values, axis=-1, keepdims=True))
    centered = values - row_mean
    return centered * lax.rsqrt(lax.optimization_barrier(jnp.mean(centered * centered, axis=-1, keepdims=True)) + norm_eps)

def attend_heads(packed):
    score_scale = 1.0 / math.sqrt(HD)
    scores = low_back(jnp.einsum('qhd,khd->hqk', packed[:, 0], packed[:, 1], precision=highest) * score_scale)
    row_max = lax.optimization_barrier(jnp.max(scores, axis=-1, keepdims=True))
    exp_scores = jnp.exp(scores - row_max)
    probs = low(exp_scores / lax.optimization_barrier(jnp.sum(exp_scores, axis=-1, keepdims=True)))
    return jnp.einsum('hqk,khd->qhd', probs, packed[:, 2], precision=highest)

def layer_rows(rows, mods, params):
    qkv_weight, qv_bias, proj_weight, proj_bias, up_weight, up_bias, down_weight, down_bias = params
    latents_here = mods.shape[0]
    mod_rows = jnp.repeat(mods, SEQ, axis=0)
    shift_attn, scale_attn, gate_attn, shift_mlp, scale_mlp, gate_mlp = [mod_rows[:, column_set * D:(column_set + 1) * D] for column_set in range(6)]
    attn_input = low(norm_rows(rows) * (1.0 + scale_attn) + shift_attn)
    qkv_shift = jnp.concatenate([qv_bias[0], jnp.zeros_like(qv_bias[0]), qv_bias[1]])
    qkv_rows = low_back(low(jnp.dot(attn_input, qkv_weight.reshape(D, 3 * D), precision=highest) + qkv_shift))
    packed = qkv_rows.reshape(latents_here, SEQ, 3, H, HD)
    attn_heads = lax.map(jax.checkpoint(attend_heads), packed)
    attn_flat = low_back(low(attn_heads.reshape(latents_here * SEQ, D)))
    branch_attn = low_back(jnp.dot(attn_flat, proj_weight, precision=highest) + proj_bias)
    hidden_state = rows + gate_attn * branch_attn
    mlp_input = low(norm_rows(hidden_state) * (1.0 + scale_mlp) + shift_mlp)
    pre_act = low_back(jnp.dot(mlp_input, up_weight.T, precision=highest) + up_bias)
    hidden_low = low(jax.nn.gelu(pre_act, approximate=True))
    branch_mlp = low_back(jnp.dot(hidden_low, down_weight, precision=highest) + down_bias)
    return hidden_state + gate_mlp * branch_mlp

def reference(tokens, condition, ada_weight, ada_bias, qkv_weight, qv_bias, proj_weight, proj_bias, up_weight, up_bias, down_weight, down_bias, out_grad):
    group_size = math.gcd(LAT, 4)
    checked = jax.checkpoint(layer_rows)

    def forward(tokens_wide, cond_wide, ada_matrix, ada_offset, params):
        silu_low = low(cond_wide * jax.nn.sigmoid(cond_wide))
        mods = low_back(low(jnp.dot(silu_low, ada_matrix, precision=highest) + ada_offset))
        row_groups = tokens_wide.reshape(LAT // group_size, group_size * SEQ, D)
        mod_groups = mods.reshape(LAT // group_size, group_size, 6 * D)

        def advance(carried, element):
            return (carried, checked(element[0], element[1], params))
        unused, results = lax.scan(advance, None, (row_groups, mod_groups))
        return results.reshape(LAT * SEQ, D)
    params = tuple((array_in.astype(jnp.float32) for array_in in (qkv_weight, qv_bias, proj_weight, proj_bias, up_weight, up_bias, down_weight, down_bias)))
    primal, pullback = jax.vjp(forward, tokens.astype(jnp.float32), condition.astype(jnp.float32), ada_weight.astype(jnp.float32), ada_bias.astype(jnp.float32), params)
    tokens_grad, condition_grad, ada_weight_grad, ada_bias_grad, param_grads = pullback(out_grad.astype(jnp.float32))
    return (primal.astype(jnp.bfloat16), tokens_grad, condition_grad, ada_weight_grad, ada_bias_grad, param_grads[0], param_grads[1], param_grads[2], param_grads[3], param_grads[4], param_grads[5], param_grads[6], param_grads[7])
```

```python
import functools
import math

import jax
import jax.numpy as jnp
from jax import lax
from jax.experimental import pallas as pl
from jax.experimental.pallas import tpu as pltpu
from jax.sharding import PartitionSpec as P

D = 1024
HD = 64
SEQ = 1024
LANES = 128

norm_eps = 1e-06
score_scale = 1.0 / math.sqrt(HD)
query_block = 512
vmem_limit = 56 * 1024 * 1024


def layer_norm(values):
    row_mean = jnp.mean(values, axis=-1, keepdims=True)
    centered = values - row_mean
    inv_std = lax.rsqrt(jnp.mean(centered * centered, axis=-1, keepdims=True) + norm_eps)
    return (centered * inv_std, inv_std)


def norm_back(grad_normed, normed, inv_std):
    mean_grad = jnp.mean(grad_normed, axis=-1, keepdims=True)
    mean_cross = jnp.mean(grad_normed * normed, axis=-1, keepdims=True)
    return inv_std * (grad_normed - mean_grad - normed * mean_cross)


def gelu_tanh(values):
    return jax.nn.gelu(values, approximate=True)


def contract(left, right, left_dim, right_dim):
    return lax.dot_general(
        left, right, (((left_dim,), (right_dim,)), ((), ())), preferred_element_type=jnp.float32
    )


def head_mask(shape, head):
    lane = lax.broadcasted_iota(jnp.int32, shape, 1)
    return (lane >= head * HD) & (lane < (head + 1) * HD)


def attend_kernel(q_ref, k_ref, v_ref, out_ref, lse_ref):
    heads = LANES // HD
    keys = k_ref[...]
    values = v_ref[...]
    masks = [head_mask(keys.shape, head) for head in range(heads)]
    zero = jnp.zeros_like(keys)
    keys_of = [jnp.where(mask, keys, zero) for mask in masks]
    values_of = [jnp.where(mask, values, zero) for mask in masks]
    for start in range(0, SEQ, query_block):
        rows = pl.ds(start, query_block)
        query = q_ref[rows, :] * jnp.bfloat16(score_scale)
        total = None
        for head in range(heads):
            scores = contract(keys_of[head], query, 1, 1)
            top = jnp.max(scores, axis=0, keepdims=True)
            weights = jnp.exp(scores - top)
            norm = jnp.sum(weights, axis=0, keepdims=True)
            probs = (weights * (1.0 / norm)).astype(jnp.bfloat16)
            part = contract(probs, values_of[head], 0, 0)
            total = part if total is None else total + part
            lse_ref[0, head : head + 1, rows] = top + jnp.log(norm)
        out_ref[rows, :] = total.astype(jnp.bfloat16)


def attend_back_kernel(
    q_ref, k_ref, v_ref, do_ref, lse_ref, dq_ref, dk_ref, dv_ref, dk_acc, dv_acc
):
    heads = LANES // HD
    keys = k_ref[...]
    values = v_ref[...]
    mask_keys = [head_mask(keys.shape, head) for head in range(heads)]
    zero = jnp.zeros_like(keys)
    keys_of = [jnp.where(mask, keys, zero) for mask in mask_keys]
    values_of = [jnp.where(mask, values, zero) for mask in mask_keys]
    for start in range(0, SEQ, query_block):
        rows = pl.ds(start, query_block)
        query = q_ref[rows, :] * jnp.bfloat16(score_scale)
        grad = do_ref[rows, :]
        mask_query = [head_mask(query.shape, head) for head in range(heads)]
        none = jnp.zeros_like(query)
        total = None
        dk_new = None
        dv_new = None
        for head in range(heads):
            scores = contract(keys_of[head], query, 1, 1)
            probs = jnp.exp(scores - lse_ref[0, head : head + 1, rows])
            prob_grad = contract(values_of[head], grad, 1, 1)
            delta = jnp.sum(probs * prob_grad, axis=0, keepdims=True)
            score_grad = (probs * (prob_grad - delta)).astype(jnp.bfloat16)
            dv_part = contract(
                probs.astype(jnp.bfloat16), jnp.where(mask_query[head], grad, none), 1, 0
            )
            dk_part = contract(score_grad, jnp.where(mask_query[head], query, none), 1, 0)
            dq_part = contract(score_grad, keys_of[head], 0, 0)
            dv_new = dv_part if dv_new is None else dv_new + dv_part
            dk_new = dk_part if dk_new is None else dk_new + dk_part
            total = dq_part if total is None else total + dq_part
        dq_ref[rows, :] = (total * score_scale).astype(jnp.bfloat16)
        if start == 0:
            dk_acc[...] = dk_new
            dv_acc[...] = dv_new
        else:
            dk_acc[...] += dk_new
            dv_acc[...] += dv_new
    dk_ref[...] = dk_acc[...].astype(jnp.bfloat16)
    dv_ref[...] = dv_acc[...].astype(jnp.bfloat16)


def column_spec(offset):
    return pl.BlockSpec((SEQ, LANES), lambda step: (0, step + offset))


def attend(qkv_rows, head_cols):
    blocks = head_cols // LANES
    lse_spec = pl.BlockSpec((1, LANES // HD, SEQ), lambda step: (step, 0, 0))
    return pl.pallas_call(
        attend_kernel,
        grid=(blocks,),
        in_specs=[column_spec(0), column_spec(blocks), column_spec(2 * blocks)],
        out_specs=[column_spec(0), lse_spec],
        out_shape=[
            jax.ShapeDtypeStruct((SEQ, head_cols), jnp.bfloat16),
            jax.ShapeDtypeStruct((blocks, LANES // HD, SEQ), jnp.float32),
        ],
        compiler_params=pltpu.CompilerParams(vmem_limit_bytes=vmem_limit),
        name="attend",
    )(qkv_rows, qkv_rows, qkv_rows)


def attend_back(qkv_rows, grad_heads, lse, head_cols):
    blocks = head_cols // LANES
    lse_spec = pl.BlockSpec((1, LANES // HD, SEQ), lambda step: (step, 0, 0))
    part = jax.ShapeDtypeStruct((SEQ, head_cols), jnp.bfloat16)
    return pl.pallas_call(
        attend_back_kernel,
        grid=(blocks,),
        in_specs=[
            column_spec(0),
            column_spec(blocks),
            column_spec(2 * blocks),
            column_spec(0),
            lse_spec,
        ],
        out_specs=[column_spec(0)] * 3,
        out_shape=[part] * 3,
        scratch_shapes=[pltpu.VMEM((SEQ, LANES), jnp.float32)] * 2,
        compiler_params=pltpu.CompilerParams(vmem_limit_bytes=vmem_limit),
        name="attend_back",
    )(qkv_rows, qkv_rows, qkv_rows, grad_heads, lse)


def shards(
    dp_size,
    tensor_size,
    tokens,
    condition,
    ada_weight,
    ada_bias,
    qkv_weight,
    qv_bias,
    proj_weight,
    proj_bias,
    up_weight,
    up_bias,
    down_weight,
    down_bias,
    out_grad,
):
    rows_local = tokens.shape[0]
    pair = SEQ // rows_local
    groups = tensor_size // pair
    latents_local = condition.shape[0]
    tensor_at = lax.axis_index("tensor")
    dp_at = lax.axis_index("dp")
    f32 = jnp.float32
    bf16 = jnp.bfloat16

    def pair_move(values, step):
        moves = [(i, i // pair * pair + (i + step) % pair) for i in range(tensor_size)]
        return lax.ppermute(values, "tensor", moves)

    def group_move(values, step):
        moves = [(i, (i + step * pair) % tensor_size) for i in range(tensor_size)]
        return lax.ppermute(values, "tensor", moves)

    def pair_gather(rows):
        return jnp.concatenate([rows] + [pair_move(rows, step) for step in range(1, pair)], axis=0)

    def pair_scatter(terms):
        total = terms[:rows_local]
        for step in range(1, pair):
            piece = terms[step * rows_local : (step + 1) * rows_local].astype(bf16)
            total = total + pair_move(piece, -step).astype(f32)
        return total

    def tensor_sum(values):
        total = values
        for step in range(1, pair):
            total = total + pair_move(values, step)
        whole = total
        for step in range(1, groups):
            whole = whole + group_move(total, step)
        return whole

    def fetch_direct(weight):
        return [weight] + [group_move(weight, step) for step in range(1, groups)]

    def fetch_spread(weight):
        piece_rows = weight.shape[0] // dp_size
        piece = lax.dynamic_slice_in_dim(weight, dp_at * piece_rows, piece_rows, axis=0)
        return [weight] + [
            lax.all_gather(group_move(piece, step), "dp", axis=0, tiled=True)
            for step in range(1, groups)
        ]

    def send_home(grads):
        total = grads[0]
        for step in range(1, groups):
            total = total + group_move(grads[step].astype(bf16), -step).astype(f32)
        return total.astype(bf16)

    head_cols = qkv_weight.shape[2]
    if head_cols % LANES == 0:
        stages = [[shard] for shard in range(groups)]
    else:
        stages = [list(range(groups))]

    def joined(parts, axis):
        return parts[0] if len(parts) == 1 else jnp.concatenate(parts, axis=axis)

    qkv_of = fetch_direct(qkv_weight)
    qv_bias_of = fetch_direct(qv_bias)
    proj_of = fetch_direct(proj_weight)
    up_of = fetch_spread(up_weight)
    up_bias_of = fetch_direct(up_bias)
    down_of = fetch_spread(down_weight)

    cond_wide = condition.astype(f32)
    cond_sig = jax.nn.sigmoid(cond_wide)
    silu_low = (cond_wide * cond_sig).astype(bf16)
    silu_all = lax.all_gather(silu_low, "dp", axis=0, tiled=True)
    mod_cols = (
        jnp.dot(silu_low, ada_weight, preferred_element_type=f32) + ada_bias.astype(f32)
    ).astype(bf16)
    mod_all = lax.all_gather(mod_cols, "tensor", axis=1, tiled=True)
    mod_row = lax.dynamic_slice_in_dim(mod_all, tensor_at // pair, 1, axis=0).astype(f32)
    shift_attn, scale_attn, gate_attn, shift_mlp, scale_mlp, gate_mlp = [
        mod_row[:, column_set * D : (column_set + 1) * D] for column_set in range(6)
    ]

    tokens_wide = tokens.astype(f32)
    grad_wide = out_grad.astype(f32)
    normed_attn, inv_attn = layer_norm(tokens_wide)
    attn_input = (normed_attn * (1.0 + scale_attn) + shift_attn).astype(bf16)
    attn_pair = pair_gather(attn_input)
    grad_branch_mlp = (gate_mlp * grad_wide).astype(bf16)
    grad_pair = pair_gather(grad_branch_mlp)

    qkv_mats, qkv_rows, heads_out, heads_lse, proj_mats = [], [], [], [], []
    proj_terms = None
    for stage in stages:
        cols = head_cols * len(stage)
        weight = joined([qkv_of[s] for s in stage], 2).reshape(D, 3 * cols)
        bias = joined([qv_bias_of[s] for s in stage], 1)
        shift = jnp.concatenate([bias[0], jnp.zeros_like(bias[0]), bias[1]]).astype(f32)
        rows = (jnp.dot(attn_pair, weight, preferred_element_type=f32) + shift).astype(bf16)
        heads, lse = attend(rows, cols)
        proj = joined([proj_of[s] for s in stage], 0)
        terms = jnp.dot(heads, proj, preferred_element_type=f32)
        proj_terms = terms if proj_terms is None else proj_terms + terms
        qkv_mats.append(weight)
        qkv_rows.append(rows)
        heads_out.append(heads)
        heads_lse.append(lse)
        proj_mats.append(proj)
    branch_attn = pair_scatter(proj_terms) + proj_bias.astype(f32)
    hidden_state = tokens_wide + gate_attn * branch_attn
    normed_mlp, inv_mlp = layer_norm(hidden_state)
    mlp_input = (normed_mlp * (1.0 + scale_mlp) + shift_mlp).astype(bf16)
    mlp_pair = pair_gather(mlp_input)

    pre_acts, hiddens = [], []
    down_terms = None
    for shard in range(groups):
        pre_act = contract(mlp_pair, up_of[shard], 1, 1) + up_bias_of[shard].astype(f32)
        hidden = gelu_tanh(pre_act).astype(bf16)
        terms = jnp.dot(hidden, down_of[shard], preferred_element_type=f32)
        down_terms = terms if down_terms is None else down_terms + terms
        pre_acts.append(pre_act)
        hiddens.append(hidden)
    branch_mlp = pair_scatter(down_terms) + down_bias.astype(f32)
    block_out = (hidden_state + gate_mlp * branch_mlp).astype(bf16)

    down_grads, up_grads, up_bias_sums = [], [], []
    input_terms = None
    for shard in range(groups):
        grad_hidden = contract(grad_pair, down_of[shard], 1, 1)
        grad_pre = jax.vjp(gelu_tanh, pre_acts[shard])[1](grad_hidden)[0].astype(bf16)
        down_grads.append(contract(hiddens[shard], grad_pair, 0, 0))
        up_grads.append(contract(grad_pre, mlp_pair, 0, 0))
        up_bias_sums.append(jnp.sum(grad_pre.astype(f32), axis=0))
        terms = jnp.dot(grad_pre, up_of[shard], preferred_element_type=f32)
        input_terms = terms if input_terms is None else input_terms + terms
    down_sum = lax.psum(send_home(down_grads), "dp")
    up_home, down_sum = lax.optimization_barrier((send_home(up_grads), down_sum))
    up_sum = lax.psum(up_home, "dp")

    grad_mlp_input = pair_scatter(input_terms)
    grad_hidden_state = grad_wide + norm_back(
        grad_mlp_input * (1.0 + scale_mlp), normed_mlp, inv_mlp
    )
    grad_branch_attn = (gate_attn * grad_hidden_state).astype(bf16)
    back_pair = pair_gather(grad_branch_attn)

    proj_grads = [None] * groups
    qkv_grads = [None] * groups
    qv_sums = [None] * groups
    attn_terms = None
    for at in reversed(range(len(stages))):
        stage = stages[at]
        cols = head_cols * len(stage)
        proj_grad = contract(heads_out[at], back_pair, 0, 0)
        grad_heads = contract(back_pair, proj_mats[at], 1, 1).astype(bf16)
        parts = attend_back(qkv_rows[at], grad_heads, heads_lse[at], cols)
        grad_qkv = jnp.concatenate(parts, axis=1)
        qkv_grad = contract(attn_pair, grad_qkv, 0, 0).reshape(D, 3, cols)
        terms = contract(grad_qkv, qkv_mats[at], 1, 1)
        attn_terms = terms if attn_terms is None else attn_terms + terms
        sums = jnp.sum(grad_qkv.astype(f32), axis=0).reshape(3, cols)
        for place, shard in enumerate(stage):
            span = slice(place * head_cols, (place + 1) * head_cols)
            proj_grads[shard] = proj_grad[span]
            qkv_grads[shard] = qkv_grad[:, :, span]
            qv_sums[shard] = jnp.concatenate([sums[0, span], sums[2, span]])
    proj_home, up_sum = lax.optimization_barrier((send_home(proj_grads), up_sum))
    qkv_home = send_home(qkv_grads)

    proj_bias_part = tensor_sum(jnp.sum(grad_branch_attn.astype(f32), axis=0))
    down_bias_part = tensor_sum(jnp.sum(grad_branch_mlp.astype(f32), axis=0))
    small_own = [
        jnp.concatenate([up_bias_sums[shard], qv_sums[shard]]) for shard in range(groups)
    ]
    small_home = small_own[0]
    for step in range(1, groups):
        small_home = small_home + group_move(small_own[step], -step)
    small = jnp.concatenate([small_home, proj_bias_part, down_bias_part]).astype(bf16)

    qkv_sum, proj_sum, small_sum = lax.psum((qkv_home, proj_home, small), "dp")

    grad_attn_input = pair_scatter(attn_terms)
    tokens_grad = grad_hidden_state + norm_back(
        grad_attn_input * (1.0 + scale_attn), normed_attn, inv_attn
    )
    mod_sums = jnp.concatenate(
        [
            jnp.sum(part, axis=0)
            for part in (
                grad_attn_input,
                grad_attn_input * normed_attn,
                grad_hidden_state * branch_attn,
                grad_mlp_input,
                grad_mlp_input * normed_mlp,
                grad_wide * branch_mlp,
            )
        ]
    )
    mod_whole = mod_sums
    for step in range(1, pair):
        mod_whole = mod_whole + pair_move(mod_sums, step)
    share = 6 * D // pair
    mod_share = lax.dynamic_slice_in_dim(
        mod_whole.astype(bf16), (tensor_at % pair) * share, share, axis=0
    )
    mod_grads = lax.all_gather(mod_share[None], ("dp", "tensor"), axis=0, tiled=True)
    mod_grads = mod_grads.reshape(dp_size * latents_local, 6 * D)
    ada_cols = ada_weight.shape[1]
    mod_own = lax.dynamic_slice_in_dim(mod_grads, tensor_at * ada_cols, ada_cols, axis=1)
    ada_weight_grad = contract(silu_all, mod_own, 0, 0)
    ada_bias_grad = jnp.sum(mod_own.astype(f32), axis=0)
    mod_here = lax.dynamic_slice_in_dim(mod_own, dp_at * latents_local, latents_local, axis=0)
    silu_grad = tensor_sum(contract(mod_here, ada_weight, 1, 1))
    condition_grad = silu_grad * (cond_sig * (1.0 + cond_wide * (1.0 - cond_sig)))

    ff_local = up_weight.shape[0]
    small_sum = small_sum.astype(f32)
    at_qv = ff_local
    at_proj = at_qv + 2 * head_cols
    return (
        block_out,
        tokens_grad,
        condition_grad,
        ada_weight_grad,
        ada_bias_grad,
        qkv_sum.astype(f32),
        small_sum[at_qv:at_proj].reshape(2, head_cols),
        proj_sum.astype(f32),
        small_sum[at_proj : at_proj + D],
        up_sum.astype(f32),
        small_sum[:ff_local],
        down_sum.astype(f32),
        small_sum[at_proj + D : at_proj + 2 * D],
    )


def solution(mesh):
    placed = (
        P(("dp", "tensor"), None),
        P("dp", None),
        P(None, "tensor"),
        P("tensor"),
        P(None, None, "tensor"),
        P(None, "tensor"),
        P("tensor", None),
        P(),
        P("tensor", None),
        P("tensor"),
        P("tensor", None),
        P(),
        P(("dp", "tensor"), None),
    )
    return jax.shard_map(
        functools.partial(shards, mesh.shape["dp"], mesh.shape["tensor"]),
        mesh=mesh,
        in_specs=placed,
        out_specs=(
            P(("dp", "tensor"), None),
            P(("dp", "tensor"), None),
            P("dp", None),
            P(None, "tensor"),
            P("tensor"),
            P(None, None, "tensor"),
            P(None, "tensor"),
            P("tensor", None),
            P(),
            P("tensor", None),
            P("tensor"),
            P("tensor", None),
            P(),
        ),
        check_vma=False,
    )
```

```python
import functools
import math

import jax
import jax.numpy as jnp
from jax import lax
from jax.experimental import pallas as pl
from jax.experimental.pallas import tpu as pltpu
from jax.sharding import PartitionSpec as P

D = 1024
HD = 64
SEQ = 1024
LANES = 128

norm_eps = 1e-06
score_scale = 1.0 / math.sqrt(HD)
query_block = 512
vmem_limit = 56 * 1024 * 1024


def layer_norm(values):
    row_mean = jnp.mean(values, axis=-1, keepdims=True)
    centered = values - row_mean
    inv_std = lax.rsqrt(jnp.mean(centered * centered, axis=-1, keepdims=True) + norm_eps)
    return (centered * inv_std, inv_std)


def norm_back(grad_normed, normed, inv_std):
    mean_grad = jnp.mean(grad_normed, axis=-1, keepdims=True)
    mean_cross = jnp.mean(grad_normed * normed, axis=-1, keepdims=True)
    return inv_std * (grad_normed - mean_grad - normed * mean_cross)


def gelu_tanh(values):
    return jax.nn.gelu(values, approximate=True)


def contract(left, right, left_dim, right_dim):
    return lax.dot_general(
        left, right, (((left_dim,), (right_dim,)), ((), ())), preferred_element_type=jnp.float32
    )


def head_mask(shape, head):
    lane = lax.broadcasted_iota(jnp.int32, shape, 1)
    return (lane >= head * HD) & (lane < (head + 1) * HD)


def attend_kernel(qkv_ref, out_ref, lse_ref):
    heads = LANES // HD
    keys = qkv_ref[:, LANES : 2 * LANES]
    values = qkv_ref[:, 2 * LANES :]
    masks = [head_mask(keys.shape, head) for head in range(heads)]
    zero = jnp.zeros_like(keys)
    keys_of = [jnp.where(mask, keys, zero) for mask in masks]
    values_of = [jnp.where(mask, values, zero) for mask in masks]
    for start in range(0, SEQ, query_block):
        rows = pl.ds(start, query_block)
        query = qkv_ref[rows, :LANES] * jnp.bfloat16(score_scale)
        total = None
        for head in range(heads):
            scores = contract(keys_of[head], query, 1, 1)
            top = jnp.max(scores, axis=0, keepdims=True)
            weights = jnp.exp(scores - top)
            norm = jnp.sum(weights, axis=0, keepdims=True)
            probs = (weights * (1.0 / norm)).astype(jnp.bfloat16)
            part = contract(probs, values_of[head], 0, 0)
            total = part if total is None else total + part
            lse_ref[0, head : head + 1, rows] = top + jnp.log(norm)
        out_ref[rows, :] = total.astype(jnp.bfloat16)


def attend_back_kernel(qkv_ref, do_ref, lse_ref, dqkv_ref, dk_acc, dv_acc):
    heads = LANES // HD
    keys = qkv_ref[:, LANES : 2 * LANES]
    values = qkv_ref[:, 2 * LANES :]
    mask_keys = [head_mask(keys.shape, head) for head in range(heads)]
    zero = jnp.zeros_like(keys)
    keys_of = [jnp.where(mask, keys, zero) for mask in mask_keys]
    values_of = [jnp.where(mask, values, zero) for mask in mask_keys]
    for start in range(0, SEQ, query_block):
        rows = pl.ds(start, query_block)
        query = qkv_ref[rows, :LANES] * jnp.bfloat16(score_scale)
        grad = do_ref[rows, :]
        mask_query = [head_mask(query.shape, head) for head in range(heads)]
        none = jnp.zeros_like(query)
        total = None
        dk_new = None
        dv_new = None
        for head in range(heads):
            scores = contract(keys_of[head], query, 1, 1)
            probs = jnp.exp(scores - lse_ref[0, head : head + 1, rows])
            prob_grad = contract(values_of[head], grad, 1, 1)
            delta = jnp.sum(probs * prob_grad, axis=0, keepdims=True)
            score_grad = (probs * (prob_grad - delta)).astype(jnp.bfloat16)
            dv_part = contract(
                probs.astype(jnp.bfloat16), jnp.where(mask_query[head], grad, none), 1, 0
            )
            dk_part = contract(score_grad, jnp.where(mask_query[head], query, none), 1, 0)
            dq_part = contract(score_grad, keys_of[head], 0, 0)
            dv_new = dv_part if dv_new is None else dv_new + dv_part
            dk_new = dk_part if dk_new is None else dk_new + dk_part
            total = dq_part if total is None else total + dq_part
        dqkv_ref[rows, :LANES] = (total * score_scale).astype(jnp.bfloat16)
        if start == 0:
            dk_acc[...] = dk_new
            dv_acc[...] = dv_new
        else:
            dk_acc[...] += dk_new
            dv_acc[...] += dv_new
    dqkv_ref[:, LANES : 2 * LANES] = dk_acc[...].astype(jnp.bfloat16)
    dqkv_ref[:, 2 * LANES :] = dv_acc[...].astype(jnp.bfloat16)


def column_spec(width):
    return pl.BlockSpec((SEQ, width), lambda step: (0, step))


lse_spec = pl.BlockSpec((1, LANES // HD, SEQ), lambda step: (step, 0, 0))


def attend(qkv_rows):
    blocks = qkv_rows.shape[1] // (3 * LANES)
    return pl.pallas_call(
        attend_kernel,
        grid=(blocks,),
        in_specs=[column_spec(3 * LANES)],
        out_specs=[column_spec(LANES), lse_spec],
        out_shape=[
            jax.ShapeDtypeStruct((SEQ, blocks * LANES), jnp.bfloat16),
            jax.ShapeDtypeStruct((blocks, LANES // HD, SEQ), jnp.float32),
        ],
        compiler_params=pltpu.CompilerParams(vmem_limit_bytes=vmem_limit),
        name="attend",
    )(qkv_rows)


def attend_back(qkv_rows, grad_heads, lse):
    blocks = qkv_rows.shape[1] // (3 * LANES)
    return pl.pallas_call(
        attend_back_kernel,
        grid=(blocks,),
        in_specs=[column_spec(3 * LANES), column_spec(LANES), lse_spec],
        out_specs=column_spec(3 * LANES),
        out_shape=jax.ShapeDtypeStruct(qkv_rows.shape, jnp.bfloat16),
        scratch_shapes=[pltpu.VMEM((SEQ, LANES), jnp.float32)] * 2,
        compiler_params=pltpu.CompilerParams(vmem_limit_bytes=vmem_limit),
        name="attend_back",
    )(qkv_rows, grad_heads, lse)


def shards(
    dp_size,
    tensor_size,
    tokens,
    condition,
    ada_weight,
    ada_bias,
    qkv_weight,
    qv_bias,
    proj_weight,
    proj_bias,
    up_weight,
    up_bias,
    down_weight,
    down_bias,
    out_grad,
):
    rows_local = tokens.shape[0]
    pair = SEQ // rows_local
    groups = tensor_size // pair
    latents_local = condition.shape[0]
    tensor_at = lax.axis_index("tensor")
    dp_at = lax.axis_index("dp")
    f32 = jnp.float32
    bf16 = jnp.bfloat16

    def pair_move(values, step):
        moves = [(i, i // pair * pair + (i + step) % pair) for i in range(tensor_size)]
        return lax.ppermute(values, "tensor", moves)

    def group_move(values, step):
        moves = [(i, (i + step * pair) % tensor_size) for i in range(tensor_size)]
        return lax.ppermute(values, "tensor", moves)

    def pair_gather(rows):
        return jnp.concatenate([rows] + [pair_move(rows, step) for step in range(1, pair)], axis=0)

    def pair_scatter(terms):
        total = terms[:rows_local]
        for step in range(1, pair):
            piece = terms[step * rows_local : (step + 1) * rows_local].astype(bf16)
            total = total + pair_move(piece, -step).astype(f32)
        return total

    def tensor_sum(values):
        total = values
        for step in range(1, pair):
            total = total + pair_move(values, step)
        whole = total
        for step in range(1, groups):
            whole = whole + group_move(total, step)
        return whole

    def fetch_direct(weight):
        return [weight] + [group_move(weight, step) for step in range(1, groups)]

    def spread_pieces(weight):
        piece_rows = weight.shape[0] // dp_size
        piece = lax.dynamic_slice_in_dim(weight, dp_at * piece_rows, piece_rows, axis=0)
        return [group_move(piece, step) for step in range(1, groups)]

    def spread_gather(pieces):
        return [lax.all_gather(piece, "dp", axis=0, tiled=True) for piece in pieces]

    def away(grads):
        return [group_move(grads[step].astype(bf16), -step) for step in range(1, groups)]

    def home(own, arrived):
        total = own
        for piece in arrived:
            total = total + piece.astype(f32)
        return total.astype(bf16)

    def dp_sum(values):
        part = lax.psum_scatter(values, "dp", scatter_dimension=0, tiled=True)
        return lax.all_gather(part, "dp", axis=0, tiled=True)

    def dp_gather(rows):
        step = 1
        while step < dp_size:
            moves = [(i, i ^ step) for i in range(dp_size)]
            rows = jnp.concatenate([rows, lax.ppermute(rows, "dp", moves)], axis=0)
            step *= 2
        return rows

    hold = lax.optimization_barrier

    head_cols = qkv_weight.shape[2]
    if head_cols % LANES == 0:
        stages = [[shard] for shard in range(groups)]
    else:
        stages = [list(range(groups))]

    def joined(parts, axis):
        return parts[0] if len(parts) == 1 else jnp.concatenate(parts, axis=axis)

    ff_local = up_weight.shape[0]
    if head_cols % LANES == 0:
        blocks = head_cols // LANES
        qkv_flat = qkv_weight.reshape(D, 3, blocks, LANES).swapaxes(1, 2).reshape(D, 3 * head_cols)
        qkv_of = fetch_direct(qkv_flat)
    else:
        qkv_of = fetch_direct(qkv_weight)
    proj_of = fetch_direct(proj_weight)
    small_of = fetch_direct(jnp.concatenate([up_bias, qv_bias.reshape(-1)]))
    qv_bias_of = [part[ff_local:].reshape(2, head_cols) for part in small_of]
    up_bias_of = [part[:ff_local] for part in small_of]
    up_pieces = spread_pieces(up_weight)
    down_pieces = spread_pieces(down_weight)

    cond_wide = condition.astype(f32)
    cond_sig = jax.nn.sigmoid(cond_wide)
    silu_low = (cond_wide * cond_sig).astype(bf16)
    mod_cols = (
        jnp.dot(silu_low, ada_weight, preferred_element_type=f32) + ada_bias.astype(f32)
    ).astype(bf16)
    mod_all = lax.all_gather(mod_cols, "tensor", axis=1, tiled=True)
    mod_row = lax.dynamic_slice_in_dim(mod_all, tensor_at // pair, 1, axis=0).astype(f32)
    shift_attn, scale_attn, gate_attn, shift_mlp, scale_mlp, gate_mlp = [
        mod_row[:, column_set * D : (column_set + 1) * D] for column_set in range(6)
    ]

    tokens_wide = tokens.astype(f32)
    grad_wide = out_grad.astype(f32)
    normed_attn, inv_attn = layer_norm(tokens_wide)
    attn_input = (normed_attn * (1.0 + scale_attn) + shift_attn).astype(bf16)
    attn_input, up_pieces, down_pieces = hold((attn_input, up_pieces, down_pieces))
    up_far = spread_gather(up_pieces)
    down_far = spread_gather(down_pieces)
    attn_pair = pair_gather(attn_input)
    grad_branch_mlp = (gate_mlp * grad_wide).astype(bf16)

    qkv_mats, qkv_rows, heads_out, heads_lse, proj_mats = [], [], [], [], []
    proj_terms = None
    for at, stage in enumerate(stages):
        cols = head_cols * len(stage)
        bias = joined([qv_bias_of[s] for s in stage], 1)
        shift = jnp.stack([bias[0], jnp.zeros_like(bias[0]), bias[1]]).astype(f32)
        shift = shift.reshape(3, cols // LANES, LANES).swapaxes(0, 1).reshape(3 * cols)
        if head_cols % LANES == 0:
            weight = qkv_of[stage[0]]
        else:
            weight = joined([qkv_of[s] for s in stage], 2)
            weight = weight.reshape(D, 3, cols // LANES, LANES).swapaxes(1, 2)
            weight = weight.reshape(D, 3 * cols)
        rows = (jnp.dot(attn_pair, weight, preferred_element_type=f32) + shift).astype(bf16)
        heads, lse = attend(rows)
        if at == 0 and len(stages) > 1:
            heads, qkv_of[1:], proj_of[1:], small_of = hold(
                (heads, qkv_of[1:], proj_of[1:], small_of)
            )
        if at == len(stages) - 1:
            heads, up_far, down_far = hold((heads, up_far, down_far))
        proj = joined([proj_of[s] for s in stage], 0)
        terms = jnp.dot(heads, proj, preferred_element_type=f32)
        proj_terms = terms if proj_terms is None else proj_terms + terms
        qkv_mats.append(weight)
        qkv_rows.append(rows)
        heads_out.append(heads)
        heads_lse.append(lse)
        proj_mats.append(proj)
    up_of = [up_weight] + list(up_far)
    down_of = [down_weight] + list(down_far)
    grad_pair = pair_gather(grad_branch_mlp)
    branch_attn = pair_scatter(proj_terms) + proj_bias.astype(f32)
    hidden_state = tokens_wide + gate_attn * branch_attn
    normed_mlp, inv_mlp = layer_norm(hidden_state)
    mlp_input = (normed_mlp * (1.0 + scale_mlp) + shift_mlp).astype(bf16)
    mlp_pair = pair_gather(mlp_input)

    pre_acts, hiddens = [], []
    down_terms = None
    for shard in range(groups):
        pre_act = contract(mlp_pair, up_of[shard], 1, 1) + up_bias_of[shard].astype(f32)
        hidden = gelu_tanh(pre_act).astype(bf16)
        terms = jnp.dot(hidden, down_of[shard], preferred_element_type=f32)
        down_terms = terms if down_terms is None else down_terms + terms
        pre_acts.append(pre_act)
        hiddens.append(hidden)
    branch_mlp = pair_scatter(down_terms) + down_bias.astype(f32)
    block_out = (hidden_state + gate_mlp * branch_mlp).astype(bf16)

    down_grads, up_grads, up_bias_sums = [None] * groups, [None] * groups, [None] * groups
    input_terms = None
    for shard in reversed(range(groups)):
        down_grads[shard] = contract(hiddens[shard], grad_pair, 0, 0)
    down_away = away(down_grads)
    for shard in reversed(range(groups)):
        grad_hidden = contract(grad_pair, down_of[shard], 1, 1)
        grad_pre = jax.vjp(gelu_tanh, pre_acts[shard])[1](grad_hidden)[0].astype(bf16)
        up_grads[shard] = contract(grad_pre, mlp_pair, 0, 0)
        up_bias_sums[shard] = jnp.sum(grad_pre.astype(f32), axis=0)
        terms = jnp.dot(grad_pre, up_of[shard], preferred_element_type=f32)
        input_terms = terms if input_terms is None else input_terms + terms
    up_away = away(up_grads)

    grad_mlp_input = pair_scatter(input_terms)
    grad_hidden_state = grad_wide + norm_back(
        grad_mlp_input * (1.0 + scale_mlp), normed_mlp, inv_mlp
    )
    grad_branch_attn = (gate_attn * grad_hidden_state).astype(bf16)
    back_pair = pair_gather(grad_branch_attn)
    back_pair, down_own, down_away = hold((back_pair, down_grads[0], down_away))
    down_sum = dp_sum(home(down_own, down_away))

    proj_grads = [None] * groups
    qkv_grads = [None] * groups
    qv_sums = [None] * groups
    attn_terms = None
    for at in reversed(range(len(stages))):
        stage = stages[at]
        cols = head_cols * len(stage)
        grad_heads = contract(back_pair, proj_mats[at], 1, 1).astype(bf16)
        grad_qkv = attend_back(qkv_rows[at], grad_heads, heads_lse[at])
        if at == len(stages) - 1:
            grad_qkv, up_own, up_away = hold((grad_qkv, up_grads[0], up_away))
            up_sum = dp_sum(home(up_own, up_away))
        proj_grad = contract(heads_out[at], back_pair, 0, 0)
        qkv_grad = contract(attn_pair, grad_qkv, 0, 0)
        terms = contract(grad_qkv, qkv_mats[at], 1, 1)
        attn_terms = terms if attn_terms is None else attn_terms + terms
        sums = jnp.sum(grad_qkv.astype(f32), axis=0).reshape(cols // LANES, 3, LANES)
        sums = sums.swapaxes(0, 1).reshape(3, cols)
        if len(stage) > 1:
            qkv_grad = qkv_grad.reshape(D, cols // LANES, 3, LANES).swapaxes(1, 2)
            qkv_grad = qkv_grad.reshape(D, 3, cols)
        for place, shard in enumerate(stage):
            span = slice(place * head_cols, (place + 1) * head_cols)
            proj_grads[shard] = proj_grad[span]
            qkv_grads[shard] = qkv_grad if len(stage) == 1 else qkv_grad[:, :, span]
            qv_sums[shard] = jnp.concatenate([sums[0, span], sums[2, span]])
    proj_away = away(proj_grads)
    qkv_away = away(qkv_grads)

    grad_attn_input = pair_scatter(attn_terms)
    grad_attn_input, qkv_away, proj_away = hold((grad_attn_input, qkv_away, proj_away))
    proj_sum = dp_sum(home(proj_grads[0], proj_away))
    qkv_sum = dp_sum(home(qkv_grads[0], qkv_away))
    if qkv_sum.ndim == 2:
        qkv_sum = qkv_sum.reshape(D, head_cols // LANES, 3, LANES).swapaxes(1, 2)
        qkv_sum = qkv_sum.reshape(D, 3, head_cols)
    tokens_grad = grad_hidden_state + norm_back(
        grad_attn_input * (1.0 + scale_attn), normed_attn, inv_attn
    )
    mod_sums = jnp.concatenate(
        [
            jnp.sum(part, axis=0)
            for part in (
                grad_attn_input,
                grad_attn_input * normed_attn,
                grad_hidden_state * branch_attn,
                grad_mlp_input,
                grad_mlp_input * normed_mlp,
                grad_wide * branch_mlp,
            )
        ]
    )
    ada_cols = ada_weight.shape[1]
    mod_own = jnp.zeros((latents_local, ada_cols), f32)
    latent_index = jnp.arange(latents_local, dtype=jnp.int32)[:, None]
    for step in range(tensor_size):
        target = (tensor_at + step) % tensor_size
        piece = lax.dynamic_slice_in_dim(mod_sums, target * ada_cols, ada_cols, axis=0)
        if step:
            moves = [(i, (i + step) % tensor_size) for i in range(tensor_size)]
            piece = lax.ppermute(piece, "tensor", moves)
        source = (tensor_at + tensor_size - step) % tensor_size
        mod_own = mod_own + jnp.where(latent_index == source // pair, piece[None], 0.0)
    mod_own = mod_own.astype(bf16)
    silu_grad = tensor_sum(contract(mod_own, ada_weight, 1, 1))
    condition_grad = silu_grad * (cond_sig * (1.0 + cond_wide * (1.0 - cond_sig)))

    bias_sums = tensor_sum(
        jnp.stack(
            [
                jnp.sum(grad_branch_attn.astype(f32), axis=0),
                jnp.sum(grad_branch_mlp.astype(f32), axis=0),
            ]
        )
    )
    small_own = [
        jnp.concatenate([up_bias_sums[shard], qv_sums[shard]]) for shard in range(groups)
    ]
    small = small_own[0]
    for step in range(1, groups):
        small = small + group_move(small_own[step], -step)
    small = jnp.concatenate([small, bias_sums.reshape(-1)])
    small_size = small.shape[0]
    pad = -small_size % (latents_local * LANES)
    small = jnp.pad(small, (0, pad)).astype(bf16).reshape(latents_local, -1)
    gathered = dp_gather(jnp.concatenate([silu_low, mod_own, small], axis=1))
    silu_all = gathered[:, :D]
    mod_all_own = gathered[:, D : D + ada_cols]
    ada_weight_grad = contract(silu_all, mod_all_own, 0, 0)
    ada_bias_grad = jnp.sum(mod_all_own.astype(f32), axis=0)
    small_sum = jnp.sum(
        gathered[:, D + ada_cols :].astype(f32).reshape(dp_size, -1), axis=0
    )[:small_size]

    at_qv = ff_local
    at_proj = at_qv + 2 * head_cols
    return (
        block_out,
        tokens_grad,
        condition_grad,
        ada_weight_grad,
        ada_bias_grad,
        qkv_sum.astype(f32),
        small_sum[at_qv:at_proj].reshape(2, head_cols),
        proj_sum.astype(f32),
        small_sum[at_proj : at_proj + D],
        up_sum.astype(f32),
        small_sum[:ff_local],
        down_sum.astype(f32),
        small_sum[at_proj + D : at_proj + 2 * D],
    )


def solution(mesh):
    placed = (
        P(("dp", "tensor"), None),
        P("dp", None),
        P(None, "tensor"),
        P("tensor"),
        P(None, None, "tensor"),
        P(None, "tensor"),
        P("tensor", None),
        P(),
        P("tensor", None),
        P("tensor"),
        P("tensor", None),
        P(),
        P(("dp", "tensor"), None),
    )
    return jax.shard_map(
        functools.partial(shards, mesh.shape["dp"], mesh.shape["tensor"]),
        mesh=mesh,
        in_specs=placed,
        out_specs=(
            P(("dp", "tensor"), None),
            P(("dp", "tensor"), None),
            P("dp", None),
            P(None, "tensor"),
            P("tensor"),
            P(None, None, "tensor"),
            P(None, "tensor"),
            P("tensor", None),
            P(),
            P("tensor", None),
            P("tensor"),
            P("tensor", None),
            P(),
        ),
        check_vma=False,
    )
```

```python
import functools
import math

import jax
import jax.numpy as jnp
from jax import lax
from jax.experimental import pallas as pl
from jax.experimental.pallas import tpu as pltpu
from jax.sharding import PartitionSpec as P

D = 1024
HD = 64
SEQ = 1024
LANES = 128

norm_eps = 1e-06
score_scale = 1.0 / math.sqrt(HD)
query_block = 512
vmem_limit = 56 * 1024 * 1024


def layer_norm(values):
    row_mean = jnp.mean(values, axis=-1, keepdims=True)
    centered = values - row_mean
    inv_std = lax.rsqrt(jnp.mean(centered * centered, axis=-1, keepdims=True) + norm_eps)
    return (centered * inv_std, inv_std)


def norm_back(grad_normed, normed, inv_std):
    mean_grad = jnp.mean(grad_normed, axis=-1, keepdims=True)
    mean_cross = jnp.mean(grad_normed * normed, axis=-1, keepdims=True)
    return inv_std * (grad_normed - mean_grad - normed * mean_cross)


def gelu_tanh(values):
    return jax.nn.gelu(values, approximate=True)


def contract(left, right, left_dim, right_dim):
    return lax.dot_general(
        left, right, (((left_dim,), (right_dim,)), ((), ())), preferred_element_type=jnp.float32
    )


def head_mask(shape, head):
    lane = lax.broadcasted_iota(jnp.int32, shape, 1)
    return (lane >= head * HD) & (lane < (head + 1) * HD)


def attend_kernel(qkv_ref, out_ref, lse_ref):
    heads = LANES // HD
    keys = qkv_ref[:, LANES : 2 * LANES]
    values = qkv_ref[:, 2 * LANES :]
    masks = [head_mask(keys.shape, head) for head in range(heads)]
    zero = jnp.zeros_like(keys)
    keys_of = [jnp.where(mask, keys, zero) for mask in masks]
    values_of = [jnp.where(mask, values, zero) for mask in masks]
    for start in range(0, SEQ, query_block):
        rows = pl.ds(start, query_block)
        query = qkv_ref[rows, :LANES] * jnp.bfloat16(score_scale)
        total = None
        for head in range(heads):
            scores = contract(keys_of[head], query, 1, 1)
            top = jnp.max(scores, axis=0, keepdims=True)
            weights = jnp.exp(scores - top)
            norm = jnp.sum(weights, axis=0, keepdims=True)
            probs = (weights * (1.0 / norm)).astype(jnp.bfloat16)
            part = contract(probs, values_of[head], 0, 0)
            total = part if total is None else total + part
            lse_ref[0, head : head + 1, rows] = top + jnp.log(norm)
        out_ref[rows, :] = total.astype(jnp.bfloat16)


def attend_back_kernel(qkv_ref, do_ref, lse_ref, dqkv_ref, dk_acc, dv_acc):
    heads = LANES // HD
    keys = qkv_ref[:, LANES : 2 * LANES]
    values = qkv_ref[:, 2 * LANES :]
    mask_keys = [head_mask(keys.shape, head) for head in range(heads)]
    zero = jnp.zeros_like(keys)
    keys_of = [jnp.where(mask, keys, zero) for mask in mask_keys]
    values_of = [jnp.where(mask, values, zero) for mask in mask_keys]
    for start in range(0, SEQ, query_block):
        rows = pl.ds(start, query_block)
        query = qkv_ref[rows, :LANES] * jnp.bfloat16(score_scale)
        grad = do_ref[rows, :]
        mask_query = [head_mask(query.shape, head) for head in range(heads)]
        none = jnp.zeros_like(query)
        total = None
        dk_new = None
        dv_new = None
        for head in range(heads):
            scores = contract(keys_of[head], query, 1, 1)
            probs = jnp.exp(scores - lse_ref[0, head : head + 1, rows])
            prob_grad = contract(values_of[head], grad, 1, 1)
            delta = jnp.sum(probs * prob_grad, axis=0, keepdims=True)
            score_grad = (probs * (prob_grad - delta)).astype(jnp.bfloat16)
            dv_part = contract(
                probs.astype(jnp.bfloat16), jnp.where(mask_query[head], grad, none), 1, 0
            )
            dk_part = contract(score_grad, jnp.where(mask_query[head], query, none), 1, 0)
            dq_part = contract(score_grad, keys_of[head], 0, 0)
            dv_new = dv_part if dv_new is None else dv_new + dv_part
            dk_new = dk_part if dk_new is None else dk_new + dk_part
            total = dq_part if total is None else total + dq_part
        dqkv_ref[rows, :LANES] = (total * score_scale).astype(jnp.bfloat16)
        if start == 0:
            dk_acc[...] = dk_new
            dv_acc[...] = dv_new
        else:
            dk_acc[...] += dk_new
            dv_acc[...] += dv_new
    dqkv_ref[:, LANES : 2 * LANES] = dk_acc[...].astype(jnp.bfloat16)
    dqkv_ref[:, 2 * LANES :] = dv_acc[...].astype(jnp.bfloat16)


def column_spec(width):
    return pl.BlockSpec((SEQ, width), lambda step: (0, step))


lse_spec = pl.BlockSpec((1, LANES // HD, SEQ), lambda step: (step, 0, 0))


def attend(qkv_rows):
    blocks = qkv_rows.shape[1] // (3 * LANES)
    return pl.pallas_call(
        attend_kernel,
        grid=(blocks,),
        in_specs=[column_spec(3 * LANES)],
        out_specs=[column_spec(LANES), lse_spec],
        out_shape=[
            jax.ShapeDtypeStruct((SEQ, blocks * LANES), jnp.bfloat16),
            jax.ShapeDtypeStruct((blocks, LANES // HD, SEQ), jnp.float32),
        ],
        compiler_params=pltpu.CompilerParams(vmem_limit_bytes=vmem_limit),
        name="attend",
    )(qkv_rows)


def attend_back(qkv_rows, grad_heads, lse):
    blocks = qkv_rows.shape[1] // (3 * LANES)
    return pl.pallas_call(
        attend_back_kernel,
        grid=(blocks,),
        in_specs=[column_spec(3 * LANES), column_spec(LANES), lse_spec],
        out_specs=column_spec(3 * LANES),
        out_shape=jax.ShapeDtypeStruct(qkv_rows.shape, jnp.bfloat16),
        scratch_shapes=[pltpu.VMEM((SEQ, LANES), jnp.float32)] * 2,
        compiler_params=pltpu.CompilerParams(vmem_limit_bytes=vmem_limit),
        name="attend_back",
    )(qkv_rows, grad_heads, lse)


def shards(
    dp_size,
    tensor_size,
    tokens,
    condition,
    ada_weight,
    ada_bias,
    qkv_weight,
    qv_bias,
    proj_weight,
    proj_bias,
    up_weight,
    up_bias,
    down_weight,
    down_bias,
    out_grad,
):
    rows_local = tokens.shape[0]
    pair = SEQ // rows_local
    groups = tensor_size // pair
    latents_local = condition.shape[0]
    tensor_at = lax.axis_index("tensor")
    dp_at = lax.axis_index("dp")
    f32 = jnp.float32
    bf16 = jnp.bfloat16

    def pair_move(values, step):
        moves = [(i, i // pair * pair + (i + step) % pair) for i in range(tensor_size)]
        return lax.ppermute(values, "tensor", moves)

    def group_move(values, step):
        moves = [(i, (i + step * pair) % tensor_size) for i in range(tensor_size)]
        return lax.ppermute(values, "tensor", moves)

    def pair_gather(rows):
        return jnp.concatenate([rows] + [pair_move(rows, step) for step in range(1, pair)], axis=0)

    def pair_scatter(terms):
        total = terms[:rows_local]
        for step in range(1, pair):
            piece = terms[step * rows_local : (step + 1) * rows_local].astype(bf16)
            total = total + pair_move(piece, -step).astype(f32)
        return total

    def tensor_sum(values):
        total = values
        for step in range(1, pair):
            total = total + pair_move(values, step)
        whole = total
        for step in range(1, groups):
            whole = whole + group_move(total, step)
        return whole

    def fetch_direct(weight):
        return [weight] + [group_move(weight, step) for step in range(1, groups)]

    def spread_pieces(weights):
        piece_rows = weights[0].shape[0] // dp_size
        pieces = [
            lax.dynamic_slice_in_dim(weight, dp_at * piece_rows, piece_rows, axis=0)
            for weight in weights
        ]
        piece = jnp.concatenate(pieces, axis=1)
        return [group_move(piece, step) for step in range(1, groups)]

    def spread_gather(pieces):
        return [lax.all_gather(piece, "dp", axis=0, tiled=True) for piece in pieces]

    def away(grads):
        return [group_move(grads[step].astype(bf16), -step) for step in range(1, groups)]

    def home(own, arrived):
        total = own
        for piece in arrived:
            total = total + piece.astype(f32)
        return total.astype(bf16)

    def dp_move(values, bit):
        return lax.ppermute(values, "dp", [(i, i ^ bit) for i in range(dp_size)])

    bits = [1 << at for at in range(dp_size.bit_length() - 1)]
    turned = bits[1:] + bits[:1]

    def dp_sum(values, order):
        part = values
        for bit in order:
            half = part.shape[0] // 2
            mine = (dp_at // bit) % 2
            keep = lax.dynamic_slice_in_dim(part, mine * half, half, axis=0)
            give = lax.dynamic_slice_in_dim(part, (1 - mine) * half, half, axis=0)
            part = (keep.astype(f32) + dp_move(give, bit).astype(f32)).astype(bf16)
        for bit in reversed(order):
            first = (dp_at // bit) % 2 == 0
            other = dp_move(part, bit)
            part = jnp.concatenate(
                [jnp.where(first, part, other), jnp.where(first, other, part)], axis=0
            )
        return part

    def dp_gather(rows):
        for bit in bits:
            rows = jnp.concatenate([rows, dp_move(rows, bit)], axis=0)
        return rows

    hold = lax.optimization_barrier

    head_cols = qkv_weight.shape[2]
    if head_cols % LANES == 0:
        stages = [[shard] for shard in range(groups)]
    else:
        stages = [list(range(groups))]

    def joined(parts, axis):
        return parts[0] if len(parts) == 1 else jnp.concatenate(parts, axis=axis)

    ff_local = up_weight.shape[0]
    if head_cols % LANES == 0:
        blocks = head_cols // LANES
        qkv_flat = qkv_weight.reshape(D, 3, blocks, LANES).swapaxes(1, 2).reshape(D, 3 * head_cols)
        condition, qkv_flat = hold((condition, qkv_flat))
        qkv_of = fetch_direct(qkv_flat)
    else:
        qkv_of = fetch_direct(qkv_weight)
    proj_of = fetch_direct(proj_weight)
    small_of = fetch_direct(jnp.concatenate([up_bias, qv_bias.reshape(-1)]))
    far_pieces = spread_pieces([up_weight, down_weight])

    cond_wide = condition.astype(f32)
    cond_sig = jax.nn.sigmoid(cond_wide)
    silu_low = (cond_wide * cond_sig).astype(bf16)
    mod_cols = (
        jnp.dot(silu_low, ada_weight, preferred_element_type=f32) + ada_bias.astype(f32)
    ).astype(bf16)
    mod_all = lax.all_gather(mod_cols, "tensor", axis=1, tiled=True)
    mod_row = lax.dynamic_slice_in_dim(mod_all, tensor_at // pair, 1, axis=0).astype(f32)
    shift_attn, scale_attn, gate_attn, shift_mlp, scale_mlp, gate_mlp = [
        mod_row[:, column_set * D : (column_set + 1) * D] for column_set in range(6)
    ]

    tokens_wide = tokens.astype(f32)
    grad_wide = out_grad.astype(f32)
    normed_attn, inv_attn = layer_norm(tokens_wide)
    attn_input = (normed_attn * (1.0 + scale_attn) + shift_attn).astype(bf16)
    attn_input, far_pieces = hold((attn_input, far_pieces))
    far = spread_gather(far_pieces)
    attn_pair = pair_gather(attn_input)
    grad_branch_mlp = (gate_mlp * grad_wide).astype(bf16)

    qkv_mats, qkv_rows, heads_out, heads_lse, proj_mats = [], [], [], [], []
    proj_terms = None
    for at, stage in enumerate(stages):
        cols = head_cols * len(stage)
        bias = [small_of[s][ff_local:].reshape(2, head_cols) if s else qv_bias for s in stage]
        bias = joined(bias, 1)
        shift = jnp.stack([bias[0], jnp.zeros_like(bias[0]), bias[1]]).astype(f32)
        shift = shift.reshape(3, cols // LANES, LANES).swapaxes(0, 1).reshape(3 * cols)
        if head_cols % LANES == 0:
            weight = qkv_of[stage[0]]
        else:
            weight = joined([qkv_of[s] for s in stage], 2)
            weight = weight.reshape(D, 3, cols // LANES, LANES).swapaxes(1, 2)
            weight = weight.reshape(D, 3 * cols)
        rows = (jnp.dot(attn_pair, weight, preferred_element_type=f32) + shift).astype(bf16)
        heads, lse = attend(rows)
        if at == 0 and len(stages) > 1:
            heads, qkv_of[1:], proj_of[1:], small_of[1:] = hold(
                (heads, qkv_of[1:], proj_of[1:], small_of[1:])
            )
        if at == len(stages) - 1:
            heads, far = hold((heads, far))
        proj = joined([proj_of[s] for s in stage], 0)
        terms = jnp.dot(heads, proj, preferred_element_type=f32)
        proj_terms = terms if proj_terms is None else proj_terms + terms
        qkv_mats.append(weight)
        qkv_rows.append(rows)
        heads_out.append(heads)
        heads_lse.append(lse)
        proj_mats.append(proj)
    up_of = [up_weight] + [part[:, :D] for part in far]
    down_of = [down_weight] + [part[:, D:] for part in far]
    up_bias_of = [up_bias] + [part[:ff_local] for part in small_of[1:]]
    grad_pair = pair_gather(grad_branch_mlp)
    branch_attn = pair_scatter(proj_terms) + proj_bias.astype(f32)
    hidden_state = tokens_wide + gate_attn * branch_attn
    normed_mlp, inv_mlp = layer_norm(hidden_state)
    mlp_input = (normed_mlp * (1.0 + scale_mlp) + shift_mlp).astype(bf16)
    mlp_pair = pair_gather(mlp_input)

    pre_acts, hiddens = [], []
    down_terms = None
    for shard in range(groups):
        pre_act = contract(mlp_pair, up_of[shard], 1, 1) + up_bias_of[shard].astype(f32)
        hidden = gelu_tanh(pre_act).astype(bf16)
        terms = jnp.dot(hidden, down_of[shard], preferred_element_type=f32)
        down_terms = terms if down_terms is None else down_terms + terms
        pre_acts.append(pre_act)
        hiddens.append(hidden)
    branch_mlp = pair_scatter(down_terms) + down_bias.astype(f32)
    block_out = (hidden_state + gate_mlp * branch_mlp).astype(bf16)

    down_grads, up_grads, up_bias_sums = [None] * groups, [None] * groups, [None] * groups
    input_terms = None
    for shard in reversed(range(groups)):
        down_grads[shard] = contract(hiddens[shard], grad_pair, 0, 0)
    down_away = away(down_grads)
    for shard in reversed(range(groups)):
        grad_hidden = contract(grad_pair, down_of[shard], 1, 1)
        grad_pre = jax.vjp(gelu_tanh, pre_acts[shard])[1](grad_hidden)[0].astype(bf16)
        up_grads[shard] = contract(grad_pre, mlp_pair, 0, 0)
        up_bias_sums[shard] = jnp.sum(grad_pre.astype(f32), axis=0)
        terms = jnp.dot(grad_pre, up_of[shard], preferred_element_type=f32)
        input_terms = terms if input_terms is None else input_terms + terms
    up_away = away(up_grads)

    grad_mlp_input = pair_scatter(input_terms)
    grad_hidden_state = grad_wide + norm_back(
        grad_mlp_input * (1.0 + scale_mlp), normed_mlp, inv_mlp
    )
    grad_branch_attn = (gate_attn * grad_hidden_state).astype(bf16)
    back_pair = pair_gather(grad_branch_attn)

    proj_grads = [None] * groups
    qkv_grads = [None] * groups
    qv_sums = [None] * groups
    attn_terms = None
    for at in reversed(range(len(stages))):
        stage = stages[at]
        cols = head_cols * len(stage)
        grad_heads = contract(back_pair, proj_mats[at], 1, 1).astype(bf16)
        grad_qkv = attend_back(qkv_rows[at], grad_heads, heads_lse[at])
        if at == len(stages) - 1:
            grad_qkv, down_own, down_away = hold((grad_qkv, down_grads[0], down_away))
            down_sum = dp_sum(home(down_own, down_away), bits)
        if at == 0:
            grad_qkv, up_own, up_away = hold((grad_qkv, up_grads[0], up_away))
            up_sum = dp_sum(home(up_own, up_away), turned)
        proj_grad = contract(back_pair, heads_out[at], 0, 0)
        qkv_grad = contract(attn_pair, grad_qkv, 0, 0)
        terms = contract(grad_qkv, qkv_mats[at], 1, 1)
        attn_terms = terms if attn_terms is None else attn_terms + terms
        sums = jnp.sum(grad_qkv.astype(f32), axis=0).reshape(cols // LANES, 3, LANES)
        sums = sums.swapaxes(0, 1).reshape(3, cols)
        if len(stage) > 1:
            qkv_grad = qkv_grad.reshape(D, cols // LANES, 3, LANES).swapaxes(1, 2)
            qkv_grad = qkv_grad.reshape(D, 3, cols)
        for place, shard in enumerate(stage):
            span = slice(place * head_cols, (place + 1) * head_cols)
            proj_grads[shard] = proj_grad[:, span]
            part = qkv_grad if len(stage) == 1 else qkv_grad[:, :, span].reshape(D, -1)
            qkv_grads[shard] = part
            qv_sums[shard] = jnp.concatenate([sums[0, span], sums[2, span]])
    proj_away = away(proj_grads)
    qkv_away = away(qkv_grads)

    grad_attn_input = pair_scatter(attn_terms)
    grad_attn_input, qkv_away, proj_away = hold((grad_attn_input, qkv_away, proj_away))
    attn_home = jnp.concatenate(
        [home(qkv_grads[0], qkv_away), home(proj_grads[0], proj_away)], axis=1
    )
    middle = attn_home.shape[1] // 2
    attn_sum = jnp.concatenate(
        [dp_sum(attn_home[:, :middle], bits), dp_sum(attn_home[:, middle:], turned)], axis=1
    )
    qkv_sum = attn_sum[:, : 3 * head_cols]
    proj_sum = attn_sum[:, 3 * head_cols :].T
    if len(stages[0]) > 1:
        qkv_sum = qkv_sum.reshape(D, 3, head_cols)
    else:
        qkv_sum = qkv_sum.reshape(D, head_cols // LANES, 3, LANES).swapaxes(1, 2)
        qkv_sum = qkv_sum.reshape(D, 3, head_cols)
    tokens_grad = grad_hidden_state + norm_back(
        grad_attn_input * (1.0 + scale_attn), normed_attn, inv_attn
    )
    mod_sums = jnp.concatenate(
        [
            jnp.sum(part, axis=0)
            for part in (
                grad_attn_input,
                grad_attn_input * normed_attn,
                grad_hidden_state * branch_attn,
                grad_mlp_input,
                grad_mlp_input * normed_mlp,
                grad_wide * branch_mlp,
            )
        ]
    )
    ada_cols = ada_weight.shape[1]
    mod_own = jnp.zeros((latents_local, ada_cols), f32)
    latent_index = jnp.arange(latents_local, dtype=jnp.int32)[:, None]
    for step in range(tensor_size):
        target = (tensor_at + step) % tensor_size
        piece = lax.dynamic_slice_in_dim(mod_sums, target * ada_cols, ada_cols, axis=0)
        if step:
            moves = [(i, (i + step) % tensor_size) for i in range(tensor_size)]
            piece = lax.ppermute(piece, "tensor", moves)
        source = (tensor_at + tensor_size - step) % tensor_size
        mod_own = mod_own + jnp.where(latent_index == source // pair, piece[None], 0.0)
    mod_own = mod_own.astype(bf16)
    silu_grad = tensor_sum(contract(mod_own, ada_weight, 1, 1))
    condition_grad = silu_grad * (cond_sig * (1.0 + cond_wide * (1.0 - cond_sig)))

    bias_sums = tensor_sum(
        jnp.stack(
            [
                jnp.sum(grad_branch_attn.astype(f32), axis=0),
                jnp.sum(grad_branch_mlp.astype(f32), axis=0),
            ]
        )
    )
    small_own = [
        jnp.concatenate([up_bias_sums[shard], qv_sums[shard]]) for shard in range(groups)
    ]
    small = small_own[0]
    for step in range(1, groups):
        small = small + group_move(small_own[step], -step)
    small = jnp.concatenate([small, bias_sums.reshape(-1)])
    small_size = small.shape[0]
    pad = -small_size % (latents_local * LANES)
    small = jnp.pad(small, (0, pad)).astype(bf16).reshape(latents_local, -1)
    gathered = dp_gather(jnp.concatenate([silu_low, mod_own, small], axis=1))
    silu_all = gathered[:, :D]
    mod_all_own = gathered[:, D : D + ada_cols]
    ada_weight_grad = contract(silu_all, mod_all_own, 0, 0)
    ada_bias_grad = jnp.sum(mod_all_own.astype(f32), axis=0)
    small_sum = jnp.sum(
        gathered[:, D + ada_cols :].astype(f32).reshape(dp_size, -1), axis=0
    )[:small_size]

    at_qv = ff_local
    at_proj = at_qv + 2 * head_cols
    return (
        block_out,
        tokens_grad,
        condition_grad,
        ada_weight_grad,
        ada_bias_grad,
        qkv_sum.astype(f32),
        small_sum[at_qv:at_proj].reshape(2, head_cols),
        proj_sum.astype(f32),
        small_sum[at_proj : at_proj + D],
        up_sum.astype(f32),
        small_sum[:ff_local],
        down_sum.astype(f32),
        small_sum[at_proj + D : at_proj + 2 * D],
    )


def solution(mesh):
    placed = (
        P(("dp", "tensor"), None),
        P("dp", None),
        P(None, "tensor"),
        P("tensor"),
        P(None, None, "tensor"),
        P(None, "tensor"),
        P("tensor", None),
        P(),
        P("tensor", None),
        P("tensor"),
        P("tensor", None),
        P(),
        P(("dp", "tensor"), None),
    )
    return jax.shard_map(
        functools.partial(shards, mesh.shape["dp"], mesh.shape["tensor"]),
        mesh=mesh,
        in_specs=placed,
        out_specs=(
            P(("dp", "tensor"), None),
            P(("dp", "tensor"), None),
            P("dp", None),
            P(None, "tensor"),
            P("tensor"),
            P(None, None, "tensor"),
            P(None, "tensor"),
            P("tensor", None),
            P(),
            P("tensor", None),
            P("tensor"),
            P("tensor", None),
            P(),
        ),
        check_vma=False,
    )
```

```python
import functools
import math

import jax
import jax.numpy as jnp
from jax import lax
from jax.experimental import pallas as pl
from jax.experimental.pallas import tpu as pltpu
from jax.sharding import PartitionSpec as P

D = 1024
HD = 64
SEQ = 1024
LANES = 128

norm_eps = 1e-06
score_scale = 1.0 / math.sqrt(HD)
query_block = 512
vmem_limit = 56 * 1024 * 1024


def layer_norm(values):
    row_mean = jnp.mean(values, axis=-1, keepdims=True)
    centered = values - row_mean
    inv_std = lax.rsqrt(jnp.mean(centered * centered, axis=-1, keepdims=True) + norm_eps)
    return (centered * inv_std, inv_std)


def norm_back(grad_normed, normed, inv_std):
    mean_grad = jnp.mean(grad_normed, axis=-1, keepdims=True)
    mean_cross = jnp.mean(grad_normed * normed, axis=-1, keepdims=True)
    return inv_std * (grad_normed - mean_grad - normed * mean_cross)


def gelu_tanh(values):
    return jax.nn.gelu(values, approximate=True)


def contract(left, right, left_dim, right_dim):
    return lax.dot_general(
        left, right, (((left_dim,), (right_dim,)), ((), ())), preferred_element_type=jnp.float32
    )


def head_mask(shape, head):
    lane = lax.broadcasted_iota(jnp.int32, shape, 1)
    return (lane >= head * HD) & (lane < (head + 1) * HD)


def attend_kernel(qkv_ref, out_ref, lse_ref):
    heads = LANES // HD
    keys = qkv_ref[:, LANES : 2 * LANES]
    values = qkv_ref[:, 2 * LANES :]
    masks = [head_mask(keys.shape, head) for head in range(heads)]
    zero = jnp.zeros_like(keys)
    keys_of = [jnp.where(mask, keys, zero) for mask in masks]
    values_of = [jnp.where(mask, values, zero) for mask in masks]
    for start in range(0, SEQ, query_block):
        rows = pl.ds(start, query_block)
        query = qkv_ref[rows, :LANES] * jnp.bfloat16(score_scale)
        total = None
        for head in range(heads):
            scores = contract(keys_of[head], query, 1, 1)
            top = jnp.max(scores, axis=0, keepdims=True)
            weights = jnp.exp(scores - top)
            norm = jnp.sum(weights, axis=0, keepdims=True)
            probs = (weights * (1.0 / norm)).astype(jnp.bfloat16)
            part = contract(probs, values_of[head], 0, 0)
            total = part if total is None else total + part
            lse_ref[0, head : head + 1, rows] = top + jnp.log(norm)
        out_ref[rows, :] = total.astype(jnp.bfloat16)


def attend_back_kernel(qkv_ref, do_ref, lse_ref, dqkv_ref, dk_acc, dv_acc):
    heads = LANES // HD
    keys = qkv_ref[:, LANES : 2 * LANES]
    values = qkv_ref[:, 2 * LANES :]
    mask_keys = [head_mask(keys.shape, head) for head in range(heads)]
    zero = jnp.zeros_like(keys)
    keys_of = [jnp.where(mask, keys, zero) for mask in mask_keys]
    values_of = [jnp.where(mask, values, zero) for mask in mask_keys]
    for start in range(0, SEQ, query_block):
        rows = pl.ds(start, query_block)
        query = qkv_ref[rows, :LANES] * jnp.bfloat16(score_scale)
        grad = do_ref[rows, :]
        mask_query = [head_mask(query.shape, head) for head in range(heads)]
        none = jnp.zeros_like(query)
        total = None
        dk_new = None
        dv_new = None
        for head in range(heads):
            scores = contract(keys_of[head], query, 1, 1)
            probs = jnp.exp(scores - lse_ref[0, head : head + 1, rows])
            prob_grad = contract(values_of[head], grad, 1, 1)
            delta = jnp.sum(probs * prob_grad, axis=0, keepdims=True)
            score_grad = (probs * (prob_grad - delta)).astype(jnp.bfloat16)
            dv_part = contract(
                probs.astype(jnp.bfloat16), jnp.where(mask_query[head], grad, none), 1, 0
            )
            dk_part = contract(score_grad, jnp.where(mask_query[head], query, none), 1, 0)
            dq_part = contract(score_grad, keys_of[head], 0, 0)
            dv_new = dv_part if dv_new is None else dv_new + dv_part
            dk_new = dk_part if dk_new is None else dk_new + dk_part
            total = dq_part if total is None else total + dq_part
        dqkv_ref[rows, :LANES] = (total * score_scale).astype(jnp.bfloat16)
        if start == 0:
            dk_acc[...] = dk_new
            dv_acc[...] = dv_new
        else:
            dk_acc[...] += dk_new
            dv_acc[...] += dv_new
    dqkv_ref[:, LANES : 2 * LANES] = dk_acc[...].astype(jnp.bfloat16)
    dqkv_ref[:, 2 * LANES :] = dv_acc[...].astype(jnp.bfloat16)


def column_spec(width):
    return pl.BlockSpec((SEQ, width), lambda step: (0, step))


lse_spec = pl.BlockSpec((1, LANES // HD, SEQ), lambda step: (step, 0, 0))


def attend(qkv_rows):
    blocks = qkv_rows.shape[1] // (3 * LANES)
    return pl.pallas_call(
        attend_kernel,
        grid=(blocks,),
        in_specs=[column_spec(3 * LANES)],
        out_specs=[column_spec(LANES), lse_spec],
        out_shape=[
            jax.ShapeDtypeStruct((SEQ, blocks * LANES), jnp.bfloat16),
            jax.ShapeDtypeStruct((blocks, LANES // HD, SEQ), jnp.float32),
        ],
        compiler_params=pltpu.CompilerParams(vmem_limit_bytes=vmem_limit),
        name="attend",
    )(qkv_rows)


def attend_back(qkv_rows, grad_heads, lse):
    blocks = qkv_rows.shape[1] // (3 * LANES)
    return pl.pallas_call(
        attend_back_kernel,
        grid=(blocks,),
        in_specs=[column_spec(3 * LANES), column_spec(LANES), lse_spec],
        out_specs=column_spec(3 * LANES),
        out_shape=jax.ShapeDtypeStruct(qkv_rows.shape, jnp.bfloat16),
        scratch_shapes=[pltpu.VMEM((SEQ, LANES), jnp.float32)] * 2,
        compiler_params=pltpu.CompilerParams(vmem_limit_bytes=vmem_limit),
        name="attend_back",
    )(qkv_rows, grad_heads, lse)


def shards(
    dp_size,
    tensor_size,
    tokens,
    condition,
    ada_weight,
    ada_bias,
    qkv_weight,
    qv_bias,
    proj_weight,
    proj_bias,
    up_weight,
    up_bias,
    down_weight,
    down_bias,
    out_grad,
):
    rows_local = tokens.shape[0]
    pair = SEQ // rows_local
    groups = tensor_size // pair
    latents_local = condition.shape[0]
    tensor_at = lax.axis_index("tensor")
    dp_at = lax.axis_index("dp")
    f32 = jnp.float32
    bf16 = jnp.bfloat16

    def pair_move(values, step):
        moves = [(i, i // pair * pair + (i + step) % pair) for i in range(tensor_size)]
        return lax.ppermute(values, "tensor", moves)

    def group_move(values, step):
        moves = [(i, (i + step * pair) % tensor_size) for i in range(tensor_size)]
        return lax.ppermute(values, "tensor", moves)

    def pair_gather(rows):
        return jnp.concatenate([rows] + [pair_move(rows, step) for step in range(1, pair)], axis=0)

    def pair_scatter(terms):
        total = terms[:rows_local]
        for step in range(1, pair):
            piece = terms[step * rows_local : (step + 1) * rows_local].astype(bf16)
            total = total + pair_move(piece, -step).astype(f32)
        return total

    def tensor_sum(values):
        total = values
        for step in range(1, pair):
            total = total + pair_move(values, step)
        whole = total
        for step in range(1, groups):
            whole = whole + group_move(total, step)
        return whole

    def fetch_direct(weight):
        return [weight] + [group_move(weight, step) for step in range(1, groups)]

    def spread_pieces(weights):
        piece_rows = weights[0].shape[0] // dp_size
        pieces = [
            lax.dynamic_slice_in_dim(weight, dp_at * piece_rows, piece_rows, axis=0)
            for weight in weights
        ]
        piece = jnp.concatenate(pieces, axis=1)
        return [group_move(piece, step) for step in range(1, groups)]

    def spread_gather(pieces):
        return [lax.all_gather(piece, "dp", axis=0, tiled=True) for piece in pieces]

    def away(grads):
        return [group_move(grads[step].astype(bf16), -step) for step in range(1, groups)]

    def home(own, arrived):
        total = own
        for piece in arrived:
            total = total + piece.astype(f32)
        return total.astype(bf16)

    def dp_move(values, bit):
        return lax.ppermute(values, "dp", [(i, i ^ bit) for i in range(dp_size)])

    bits = [1 << at for at in range(dp_size.bit_length() - 1)]
    turned = bits[1:] + bits[:1]

    def dp_sum(values, order):
        part = values
        for bit in order:
            half = part.shape[0] // 2
            mine = (dp_at // bit) % 2
            keep = lax.dynamic_slice_in_dim(part, mine * half, half, axis=0)
            give = lax.dynamic_slice_in_dim(part, (1 - mine) * half, half, axis=0)
            part = (keep.astype(f32) + dp_move(give, bit).astype(f32)).astype(bf16)
        for bit in reversed(order):
            first = (dp_at // bit) % 2 == 0
            other = dp_move(part, bit)
            part = jnp.concatenate(
                [jnp.where(first, part, other), jnp.where(first, other, part)], axis=0
            )
        return part

    def dp_gather(rows):
        for bit in bits:
            rows = jnp.concatenate([rows, dp_move(rows, bit)], axis=0)
        return rows

    hold = lax.optimization_barrier

    head_cols = qkv_weight.shape[2]
    if head_cols % LANES == 0:
        stages = [[shard] for shard in range(groups)]
    else:
        stages = [list(range(groups))]

    def joined(parts, axis):
        return parts[0] if len(parts) == 1 else jnp.concatenate(parts, axis=axis)

    ff_local = up_weight.shape[0]
    small_of = fetch_direct(jnp.concatenate([up_bias, qv_bias.reshape(-1)]))
    if head_cols % LANES == 0:
        blocks = head_cols // LANES
        qkv_flat = qkv_weight.reshape(D, 3, blocks, LANES).swapaxes(1, 2).reshape(D, 3 * head_cols)
        condition, qkv_flat, proj_send, small_of[1:] = hold(
            (condition, qkv_flat, proj_weight, small_of[1:])
        )
        qkv_of = fetch_direct(qkv_flat)
    else:
        proj_send = proj_weight
        qkv_of = fetch_direct(qkv_weight)
    proj_of = [proj_weight] + fetch_direct(proj_send)[1:]
    far_pieces = spread_pieces([up_weight, down_weight])

    cond_wide = condition.astype(f32)
    cond_sig = jax.nn.sigmoid(cond_wide)
    silu_low = (cond_wide * cond_sig).astype(bf16)
    mod_cols = (
        jnp.dot(silu_low, ada_weight, preferred_element_type=f32) + ada_bias.astype(f32)
    ).astype(bf16)
    mod_all = lax.all_gather(mod_cols, "tensor", axis=1, tiled=True)
    mod_row = lax.dynamic_slice_in_dim(mod_all, tensor_at // pair, 1, axis=0).astype(f32)
    shift_attn, scale_attn, gate_attn, shift_mlp, scale_mlp, gate_mlp = [
        mod_row[:, column_set * D : (column_set + 1) * D] for column_set in range(6)
    ]

    tokens_wide = tokens.astype(f32)
    grad_wide = out_grad.astype(f32)
    normed_attn, inv_attn = layer_norm(tokens_wide)
    attn_input = (normed_attn * (1.0 + scale_attn) + shift_attn).astype(bf16)
    attn_input, far_pieces = hold((attn_input, far_pieces))
    far = spread_gather(far_pieces)
    attn_pair = pair_gather(attn_input)
    grad_branch_mlp = (gate_mlp * grad_wide).astype(bf16)

    qkv_mats, qkv_rows, heads_out, heads_lse, proj_mats = [], [], [], [], []
    proj_terms = None
    for at, stage in enumerate(stages):
        cols = head_cols * len(stage)
        bias = [small_of[s][ff_local:].reshape(2, head_cols) if s else qv_bias for s in stage]
        bias = joined(bias, 1)
        shift = jnp.stack([bias[0], jnp.zeros_like(bias[0]), bias[1]]).astype(f32)
        shift = shift.reshape(3, cols // LANES, LANES).swapaxes(0, 1).reshape(3 * cols)
        if head_cols % LANES == 0:
            weight = qkv_of[stage[0]]
        else:
            weight = joined([qkv_of[s] for s in stage], 2)
            weight = weight.reshape(D, 3, cols // LANES, LANES).swapaxes(1, 2)
            weight = weight.reshape(D, 3 * cols)
        rows = (jnp.dot(attn_pair, weight, preferred_element_type=f32) + shift).astype(bf16)
        heads, lse = attend(rows)
        if at == 0 and len(stages) > 1:
            heads, qkv_of[1:] = hold((heads, qkv_of[1:]))
        if at == len(stages) - 1:
            heads, far, proj_of[1:] = hold((heads, far, proj_of[1:]))
        proj = joined([proj_of[s] for s in stage], 0)
        terms = jnp.dot(heads, proj, preferred_element_type=f32)
        proj_terms = terms if proj_terms is None else proj_terms + terms
        qkv_mats.append(weight)
        qkv_rows.append(rows)
        heads_out.append(heads)
        heads_lse.append(lse)
        proj_mats.append(proj)
    up_of = [up_weight] + [part[:, :D] for part in far]
    down_of = [down_weight] + [part[:, D:] for part in far]
    up_bias_of = [up_bias] + [part[:ff_local] for part in small_of[1:]]
    grad_pair = pair_gather(grad_branch_mlp)
    branch_attn = pair_scatter(proj_terms) + proj_bias.astype(f32)
    hidden_state = tokens_wide + gate_attn * branch_attn
    normed_mlp, inv_mlp = layer_norm(hidden_state)
    mlp_input = (normed_mlp * (1.0 + scale_mlp) + shift_mlp).astype(bf16)
    mlp_pair = pair_gather(mlp_input)

    pre_acts, hiddens = [], []
    down_terms = None
    for shard in range(groups):
        pre_act = contract(mlp_pair, up_of[shard], 1, 1) + up_bias_of[shard].astype(f32)
        hidden = gelu_tanh(pre_act).astype(bf16)
        terms = jnp.dot(hidden, down_of[shard], preferred_element_type=f32)
        down_terms = terms if down_terms is None else down_terms + terms
        pre_acts.append(pre_act)
        hiddens.append(hidden)
    branch_mlp = pair_scatter(down_terms) + down_bias.astype(f32)
    block_out = (hidden_state + gate_mlp * branch_mlp).astype(bf16)

    down_grads, up_grads, up_bias_sums = [None] * groups, [None] * groups, [None] * groups
    input_terms = None
    for shard in reversed(range(groups)):
        down_grads[shard] = contract(hiddens[shard], grad_pair, 0, 0)
    down_away = away(down_grads)
    for shard in reversed(range(groups)):
        grad_hidden = contract(grad_pair, down_of[shard], 1, 1)
        grad_pre = jax.vjp(gelu_tanh, pre_acts[shard])[1](grad_hidden)[0].astype(bf16)
        up_grads[shard] = contract(grad_pre, mlp_pair, 0, 0)
        up_bias_sums[shard] = jnp.sum(grad_pre.astype(f32), axis=0)
        terms = jnp.dot(grad_pre, up_of[shard], preferred_element_type=f32)
        input_terms = terms if input_terms is None else input_terms + terms
    up_away = away(up_grads)

    grad_mlp_input = pair_scatter(input_terms)
    grad_hidden_state = grad_wide + norm_back(
        grad_mlp_input * (1.0 + scale_mlp), normed_mlp, inv_mlp
    )
    grad_branch_attn = (gate_attn * grad_hidden_state).astype(bf16)
    back_pair = pair_gather(grad_branch_attn)

    proj_grads = [None] * groups
    qkv_grads = [None] * groups
    qv_sums = [None] * groups
    attn_terms = None
    for at in reversed(range(len(stages))):
        stage = stages[at]
        cols = head_cols * len(stage)
        grad_heads = contract(back_pair, proj_mats[at], 1, 1).astype(bf16)
        grad_qkv = attend_back(qkv_rows[at], grad_heads, heads_lse[at])
        if at == len(stages) - 1:
            grad_qkv, down_own, down_away = hold((grad_qkv, down_grads[0], down_away))
            down_sum = dp_sum(home(down_own, down_away), bits)
        proj_grad = contract(back_pair, heads_out[at], 0, 0)
        qkv_grad = contract(attn_pair, grad_qkv, 0, 0)
        terms = contract(grad_qkv, qkv_mats[at], 1, 1)
        attn_terms = terms if attn_terms is None else attn_terms + terms
        sums = jnp.sum(grad_qkv.astype(f32), axis=0).reshape(cols // LANES, 3, LANES)
        sums = sums.swapaxes(0, 1).reshape(3, cols)
        if len(stage) > 1:
            qkv_grad = qkv_grad.reshape(D, cols // LANES, 3, LANES).swapaxes(1, 2)
            qkv_grad = qkv_grad.reshape(D, 3, cols)
        for place, shard in enumerate(stage):
            span = slice(place * head_cols, (place + 1) * head_cols)
            proj_grads[shard] = proj_grad[:, span]
            part = qkv_grad if len(stage) == 1 else qkv_grad[:, :, span].reshape(D, -1)
            qkv_grads[shard] = part
            qv_sums[shard] = jnp.concatenate([sums[0, span], sums[2, span]])
    attn_terms, up_own, up_away = hold((attn_terms, up_grads[0], up_away))
    up_sum = dp_sum(home(up_own, up_away), turned)
    proj_away = away(proj_grads)
    qkv_away = away(qkv_grads)

    grad_attn_input = pair_scatter(attn_terms)
    grad_attn_input, qkv_away, proj_away = hold((grad_attn_input, qkv_away, proj_away))
    attn_home = jnp.concatenate(
        [home(qkv_grads[0], qkv_away), home(proj_grads[0], proj_away)], axis=1
    )
    middle = attn_home.shape[1] // 2
    attn_sum = jnp.concatenate(
        [dp_sum(attn_home[:, :middle], bits), dp_sum(attn_home[:, middle:], turned)], axis=1
    )
    qkv_sum = attn_sum[:, : 3 * head_cols]
    proj_sum = attn_sum[:, 3 * head_cols :].T
    if len(stages[0]) > 1:
        qkv_sum = qkv_sum.reshape(D, 3, head_cols)
    else:
        qkv_sum = qkv_sum.reshape(D, head_cols // LANES, 3, LANES).swapaxes(1, 2)
        qkv_sum = qkv_sum.reshape(D, 3, head_cols)
    tokens_grad = grad_hidden_state + norm_back(
        grad_attn_input * (1.0 + scale_attn), normed_attn, inv_attn
    )
    mod_sums = jnp.concatenate(
        [
            jnp.sum(part, axis=0)
            for part in (
                grad_attn_input,
                grad_attn_input * normed_attn,
                grad_hidden_state * branch_attn,
                grad_mlp_input,
                grad_mlp_input * normed_mlp,
                grad_wide * branch_mlp,
            )
        ]
    )
    ada_cols = ada_weight.shape[1]
    bias_sums = jnp.concatenate(
        [
            jnp.sum(grad_branch_attn.astype(f32), axis=0),
            jnp.sum(grad_branch_mlp.astype(f32), axis=0),
        ]
    )
    bias_whole = jnp.zeros_like(bias_sums)
    small = jnp.zeros((ff_local + 2 * head_cols,), f32)
    mod_own = jnp.zeros((latents_local, ada_cols), f32)
    latent_index = jnp.arange(latents_local, dtype=jnp.int32)[:, None]
    for step in range(tensor_size):
        target = (tensor_at + step) % tensor_size
        piece = lax.dynamic_slice_in_dim(mod_sums, target * ada_cols, ada_cols, axis=0)
        piece = jnp.concatenate([piece, bias_sums])
        if step % pair == 0:
            shard = (groups - step // pair) % groups
            piece = jnp.concatenate([piece, up_bias_sums[shard], qv_sums[shard]])
        if step:
            moves = [(i, (i + step) % tensor_size) for i in range(tensor_size)]
            piece = lax.ppermute(piece, "tensor", moves)
        source = (tensor_at + tensor_size - step) % tensor_size
        mod_piece = piece[None, :ada_cols]
        mod_own = mod_own + jnp.where(latent_index == source // pair, mod_piece, 0.0)
        bias_whole = bias_whole + piece[ada_cols : ada_cols + 2 * D]
        if step % pair == 0:
            small = small + piece[ada_cols + 2 * D :]
    mod_own = mod_own.astype(bf16)
    silu_grad = tensor_sum(contract(mod_own, ada_weight, 1, 1))
    condition_grad = silu_grad * (cond_sig * (1.0 + cond_wide * (1.0 - cond_sig)))

    small = jnp.concatenate([small, bias_whole])
    small_size = small.shape[0]
    pad = -small_size % (latents_local * LANES)
    small = jnp.pad(small, (0, pad)).astype(bf16).reshape(latents_local, -1)
    gathered = dp_gather(jnp.concatenate([silu_low, mod_own, small], axis=1))
    silu_all = gathered[:, :D]
    mod_all_own = gathered[:, D : D + ada_cols]
    ada_weight_grad = contract(silu_all, mod_all_own, 0, 0)
    ada_bias_grad = jnp.sum(mod_all_own.astype(f32), axis=0)
    small_sum = jnp.sum(
        gathered[:, D + ada_cols :].astype(f32).reshape(dp_size, -1), axis=0
    )[:small_size]

    at_qv = ff_local
    at_proj = at_qv + 2 * head_cols
    return (
        block_out,
        tokens_grad,
        condition_grad,
        ada_weight_grad,
        ada_bias_grad,
        qkv_sum.astype(f32),
        small_sum[at_qv:at_proj].reshape(2, head_cols),
        proj_sum.astype(f32),
        small_sum[at_proj : at_proj + D],
        up_sum.astype(f32),
        small_sum[:ff_local],
        down_sum.astype(f32),
        small_sum[at_proj + D : at_proj + 2 * D],
    )


def solution(mesh):
    placed = (
        P(("dp", "tensor"), None),
        P("dp", None),
        P(None, "tensor"),
        P("tensor"),
        P(None, None, "tensor"),
        P(None, "tensor"),
        P("tensor", None),
        P(),
        P("tensor", None),
        P("tensor"),
        P("tensor", None),
        P(),
        P(("dp", "tensor"), None),
    )
    return jax.shard_map(
        functools.partial(shards, mesh.shape["dp"], mesh.shape["tensor"]),
        mesh=mesh,
        in_specs=placed,
        out_specs=(
            P(("dp", "tensor"), None),
            P(("dp", "tensor"), None),
            P("dp", None),
            P(None, "tensor"),
            P("tensor"),
            P(None, None, "tensor"),
            P(None, "tensor"),
            P("tensor", None),
            P(),
            P("tensor", None),
            P("tensor"),
            P("tensor", None),
            P(),
        ),
        check_vma=False,
    )
```
